32 devices in a mesh: stn: 8 (over z, x), tm: 4 (over y, core).
Axes of the slice: x: 2, y: 2, z: 4, core: 2. Of those that a mesh axis runs over, the one named last changes fastest.
Arguments:
- voltages: bfloat16 [2, 512, 262144], P(None, 'stn', 'tm'), may hold values from -6 to 6
- delays: int32 [512], P('stn'), may hold values from 0 to 2048, as said below
- fringe: int32 [512], P('stn'), may hold values from 0 to 4095
- fringe_rate: int32 [512], P('stn'), may hold values from 0 to 4095
- filter_taps: float32 [16, 1024], replicated, may hold values from -1.5 to 1.5
Outputs:
- vis_real: float32 [1024, 512, 512], P(('stn', 'tm'))
- vis_imag: float32 [1024, 512, 512], P(('stn', 'tm'))
The draws below stay inside these ranges and needn't reach their ends.
Inputs may be any that keep to these rules, and one draw needn't show every extreme that they name: `delays`: the largest delay over all stations is exactly 2048.
All inputs are finite; a program needn't handle non-finite values.
Results may differ from the reference program's by a relative error of at most 0.0066.
Values may be sent and summed in bfloat16 or wider, within the bound.
A program may use at most 448 MiB of HBM per device.

```python
import math
import jax
import jax.numpy as jnp
from jax import lax

S = 512
C = 1024
P_SIZE = 16
Q = 4096
TIME = 262144
DMAX = 2048


def draw_delays(key, part):
    key_values, key_place = jax.random.split(jax.random.fold_in(key, 7))
    values = jax.random.randint(key_values, (S,), 0, DMAX + 1)
    position = jax.random.randint(key_place, (), 0, S)
    return values.at[position].set(DMAX).astype(jnp.int32)


def set_ends(drawn, key, low, top_value):
    dims = drawn.shape
    spot = [jax.random.randint(jax.random.fold_in(key, axis), (), 0, dims[axis]) for axis in range(len(dims))]
    drawn = drawn.at[tuple(spot)].set(low)
    longest = dims.index(max(dims))
    spot[longest] = (spot[longest] + 1) % dims[longest]
    return drawn.at[tuple(spot)].set(top_value)


def levels(own_key, shape, cuts, least, high):
    loudness, own = 1.0, jax.random.fold_in(own_key, 6)
    for dim, shards_of in cuts:
        draws = jnp.exp(jax.random.uniform(jax.random.fold_in(own, dim), (shards_of,), jnp.float32, least / len(cuts), high / len(cuts)))
        loudness = loudness * jnp.repeat(draws, shape[dim] // shards_of).reshape([-1 if axis == dim else 1 for axis in range(len(shape))])
    return loudness


def scatter_about(own_key, dims, spread, most, cuts=(), kind=jnp.bfloat16):
    drawn = spread * jax.random.normal(own_key, dims, jnp.float32)
    if cuts:
        drawn = drawn * levels(own_key, dims, cuts, -0.22, 0.18)
    return jnp.clip(drawn, -most, most).astype(kind)


def setup_inputs(seed: int = 0) -> dict:
    key_list = jax.random.split(jax.random.key(seed), 6)
    voltages = scatter_about(key_list[0], (2, S, TIME), 1.0, 6.0, ((1, 8), (2, 4)))
    delays = draw_delays(jax.random.fold_in(key_list[5], 71), 0)
    fringe = set_ends(jax.random.randint(key_list[2], (S,), 0, Q), jax.random.fold_in(key_list[2], 1), 0, Q - 1).astype(jnp.int32)
    fringe_rate = set_ends(jax.random.randint(key_list[3], (S,), 0, Q), jax.random.fold_in(key_list[3], 1), 0, Q - 1).astype(jnp.int32)
    filter_taps = scatter_about(key_list[4], (P_SIZE, C), 0.25, 1.5, (), jnp.float32)
    return {"voltages": voltages, "delays": delays, "fringe": fringe, "fringe_rate": fringe_rate, "filter_taps": filter_taps}


TWO_PI = 2.0 * math.pi

def dft_tables(table_size):
    column = jnp.arange(table_size, dtype=jnp.int32)
    product = column[:, None] * column[None, :] % table_size
    angles = product.astype(jnp.float32) * (TWO_PI / table_size)
    return (jnp.cos(angles).astype(jnp.bfloat16), jnp.sin(angles).astype(jnp.bfloat16))

def transform(weighted_part, table):
    return jnp.einsum('smn,nc->csm', weighted_part.astype(jnp.float32), table.astype(jnp.float32), precision=lax.Precision.HIGHEST)

def channelize(delayed, filter_taps, fringe, fringe_rate, spectra, tables):
    stations = delayed.shape[1]
    blocks = delayed.reshape(2, stations, spectra + P_SIZE - 1, C)
    summed = jnp.zeros((2, stations, spectra, C), jnp.float32)
    for tap_index in range(P_SIZE):
        summed = summed + filter_taps[tap_index] * blocks[:, :, tap_index:tap_index + spectra].astype(jnp.float32)
    weighted = summed.astype(jnp.bfloat16)
    cosine_table, sine_table = tables
    inverse_root = 1.0 / math.sqrt(C)
    real_part = (transform(weighted[0], cosine_table) + transform(weighted[1], sine_table)) * inverse_root
    imag_part = (transform(weighted[1], cosine_table) - transform(weighted[0], sine_table)) * inverse_root
    channel = jnp.arange(C, dtype=jnp.int32)
    phase_index = (fringe[None, :] + fringe_rate[None, :] * channel[:, None]) % Q
    rotation = phase_index.astype(jnp.float32) * (TWO_PI / Q)
    rot_cos = jnp.cos(rotation)[:, :, None]
    rot_sin = jnp.sin(rotation)[:, :, None]
    out_real = real_part * rot_cos - imag_part * rot_sin
    out_imag = real_part * rot_sin + imag_part * rot_cos
    return jnp.stack([out_real, out_imag], axis=2).astype(jnp.bfloat16)

def reference(voltages, delays, fringe, fringe_rate, filter_taps):
    spectra = TIME // C
    padded = jnp.concatenate([jnp.zeros((2, S, DMAX), jnp.bfloat16), voltages, jnp.zeros((2, S, (P_SIZE - 1) * C), jnp.bfloat16)], axis=2)
    length = TIME + (P_SIZE - 1) * C
    tables = dft_tables(C)

    def select_window(station_row, delay_value):
        return lax.dynamic_slice_in_dim(station_row, (DMAX - delay_value).astype(jnp.int32), length, 1)

    def one_block(block_index):
        start = (block_index * 16).astype(jnp.int32)
        station_rows = lax.dynamic_slice_in_dim(padded, start, 16, 1)
        block_delays = lax.dynamic_slice_in_dim(delays, start, 16, 0)
        block_fringe = lax.dynamic_slice_in_dim(fringe, start, 16, 0)
        block_rate = lax.dynamic_slice_in_dim(fringe_rate, start, 16, 0)
        delayed = jax.vmap(select_window, in_axes=(1, 0), out_axes=1)(station_rows, block_delays)
        return channelize(delayed, filter_taps, block_fringe, block_rate, spectra, tables)
    stacked = lax.map(one_block, jnp.arange(S // 16, dtype=jnp.int32))

    def one_channel_block(block_index):
        start = (block_index * 8).astype(jnp.int32)
        chosen = lax.dynamic_slice_in_dim(stacked, start, 8, 1)
        left_rows = jnp.transpose(chosen, (1, 0, 2, 3, 4)).reshape(8, S, 2 * spectra).astype(jnp.float32)
        swapped = jnp.concatenate([left_rows[..., spectra:], -left_rows[..., :spectra]], axis=-1)
        gram_real = jnp.einsum('csk,cdk->csd', left_rows, left_rows, precision=lax.Precision.HIGHEST)
        gram_imag = jnp.einsum('csk,cdk->csd', swapped, left_rows, precision=lax.Precision.HIGHEST)
        return (gram_real * (1.0 / spectra), gram_imag * (1.0 / spectra))
    vis_real, vis_imag = lax.map(one_channel_block, jnp.arange(C // 8, dtype=jnp.int32))
    return (vis_real.reshape(C, S, S), vis_imag.reshape(C, S, S))
```

```python
import functools
import math

import jax
import jax.numpy as jnp
from jax import lax
from jax.experimental import pallas as pl
from jax.experimental.pallas import tpu as pltpu
from jax.sharding import PartitionSpec as P

C = 1024
P_SIZE = 16
Q = 4096
DMAX = 2048


TWO_PI = 2.0 * math.pi


def from_behind(block, axis, distance):
    devices = range(lax.axis_size(axis))
    route = [(i - distance, i) for i in devices if i - distance in devices]
    return lax.ppermute(block, axis, route)


def dft_tables(table_size):
    column = jnp.arange(table_size, dtype=jnp.int32)
    product = column[:, None] * column[None, :] % table_size
    angles = product.astype(jnp.float32) * (TWO_PI / table_size)
    return (jnp.cos(angles).astype(jnp.bfloat16), jnp.sin(angles).astype(jnp.bfloat16))


def window_filter_kernel(delay_ref, taps_ref, early_ref, main_ref, late_ref, out_ref, rolled, shifted):
    early_rows, spectra, late_rows = early_ref.shape[2], main_ref.shape[2], late_ref.shape[2]
    need = -(-(spectra + P_SIZE - 1) // 8) * 8
    start = early_rows * C - delay_ref[pl.program_id(0)]
    skip = start // C
    within = start % C
    amount = (C - within) % C
    lane = lax.broadcasted_iota(jnp.int32, (8, C), 1)
    ahead = skip + jnp.where(lane < C - within, 0, 1)
    for part in range(2):
        first = pltpu.roll(early_ref[part, 0].astype(jnp.float32), amount, 1)
        rolled[0:early_rows, :] = first[0:early_rows]
        for row in range(0, spectra, 8):
            rolled[early_rows + row : early_rows + row + 8, :] = pltpu.roll(
                main_ref[part, 0, row : row + 8, :].astype(jnp.float32), amount, 1
            )
        base = early_rows + spectra
        for row in range(0, late_rows, 8):
            rolled[base + row : base + row + 8, :] = pltpu.roll(
                late_ref[part, 0, row : row + 8, :].astype(jnp.float32), amount, 1
            )
        for row in range(0, need, 8):
            chosen = rolled[row : row + 8, :]
            for step in range(1, early_rows + 2):
                chosen = jnp.where(ahead == step, rolled[row + step : row + step + 8, :], chosen)
            shifted[row : row + 8, :] = chosen
        for left in range(0, C, 256):
            for row in range(0, spectra, 16):
                total = jnp.zeros((16, 256), jnp.float32)
                for tap in range(P_SIZE):
                    total = total + taps_ref[tap : tap + 1, left : left + 256] * shifted[
                        row + tap : row + tap + 16, left : left + 256
                    ]
                out_ref[0, part, row : row + 16, left : left + 256] = total.astype(jnp.bfloat16)


def window_filter(delays, filter_taps, early, main, late):
    stations, spectra = main.shape[1], main.shape[2]
    early_rows, late_rows = early.shape[2], late.shape[2]
    need = -(-(spectra + P_SIZE - 1) // 8) * 8
    rows = need + early_rows + 8

    def block(count):
        return pl.BlockSpec((2, 1, count, C), lambda s: (0, s, 0, 0))

    return pl.pallas_call(
        window_filter_kernel,
        grid=(stations,),
        in_specs=[
            pl.BlockSpec(memory_space=pltpu.SMEM),
            pl.BlockSpec((P_SIZE, C), lambda s: (0, 0)),
            block(early_rows),
            block(spectra),
            block(late_rows),
        ],
        out_specs=pl.BlockSpec((1, 2, spectra, C), lambda s: (s, 0, 0, 0)),
        out_shape=jax.ShapeDtypeStruct((stations, 2, spectra, C), jnp.bfloat16),
        scratch_shapes=[pltpu.VMEM((rows, C), jnp.float32), pltpu.VMEM((need, C), jnp.float32)],
    )(delays, filter_taps, early, main, late)


def channelize(weighted_rows, fringe, fringe_rate, spectra, tables):
    cosine_table, sine_table = tables
    with_cosine = jnp.einsum(
        "skn,nc->csk", weighted_rows, cosine_table, preferred_element_type=jnp.float32
    )
    with_sine = jnp.einsum(
        "skn,nc->csk", weighted_rows, sine_table, preferred_element_type=jnp.float32
    )
    inverse_root = 1.0 / math.sqrt(C)
    real_part = (with_cosine[..., :spectra] + with_sine[..., spectra:]) * inverse_root
    imag_part = (with_cosine[..., spectra:] - with_sine[..., :spectra]) * inverse_root
    channel = jnp.arange(C, dtype=jnp.int32)
    phase_index = (fringe[None, :] + fringe_rate[None, :] * channel[:, None]) % Q
    rotation = phase_index.astype(jnp.float32) * (TWO_PI / Q)
    rot_cos = jnp.cos(rotation)[:, :, None]
    rot_sin = jnp.sin(rotation)[:, :, None]
    out_real = real_part * rot_cos - imag_part * rot_sin
    out_imag = real_part * rot_sin + imag_part * rot_cos
    return jnp.concatenate([out_real, out_imag], axis=2).astype(jnp.bfloat16)


def gram_kernel(scale, spectra_ref, real_ref, imag_ref):
    stn_count, tm_count, stations, width = spectra_ref.shape[1:]
    lane = lax.broadcasted_iota(jnp.int32, (stn_count * stations, width), 1)
    pieces, turned_pieces = [], []
    for source in range(tm_count):
        piece = spectra_ref[0, :, source].reshape(stn_count * stations, width)
        turned = pltpu.roll(piece.astype(jnp.float32), width // 2, 1)
        pieces.append(piece)
        turned_pieces.append(jnp.where(lane < width // 2, turned, -turned).astype(jnp.bfloat16))
    rows = jnp.concatenate(pieces, axis=1)
    swapped = jnp.concatenate(turned_pieces, axis=1)
    last = (((1,), (1,)), ((), ()))
    real_ref[0] = lax.dot_general(rows, rows, last, preferred_element_type=jnp.float32) * scale
    imag_ref[0] = lax.dot_general(swapped, rows, last, preferred_element_type=jnp.float32) * scale


def grams(grouped, scale):
    channels, stn_count, tm_count, stations, width = grouped.shape
    whole = stn_count * stations
    result = jax.ShapeDtypeStruct((channels, whole, whole), jnp.float32)
    return pl.pallas_call(
        functools.partial(gram_kernel, scale),
        grid=(channels,),
        in_specs=[pl.BlockSpec((1, *grouped.shape[1:]), lambda c: (c, 0, 0, 0, 0))],
        out_specs=[pl.BlockSpec((1, whole, whole), lambda c: (c, 0, 0))] * 2,
        out_shape=[result, result],
    )(grouped)


def local(voltages, delays, fringe, fringe_rate, filter_taps):
    samples = voltages.shape[2]
    spectra = samples // C
    stations = voltages.shape[1]
    frames = voltages.reshape(2, stations, spectra, C)
    early = from_behind(frames[:, :, spectra - DMAX // C :], "tm", 1)
    late = from_behind(frames[:, :, :P_SIZE], "tm", -1)
    weighted = window_filter(delays, filter_taps, early, frames, late)
    weighted_rows = weighted.reshape(stations, 2 * spectra, C)
    turned = channelize(weighted_rows, fringe, fringe_rate, spectra, dft_tables(C))
    outgoing = turned.reshape(C, 1, stations, 2 * spectra)
    stn_count = lax.axis_size("stn")
    tm_count = lax.axis_size("tm")
    received = lax.all_to_all(outgoing, ("stn", "tm"), split_axis=0, concat_axis=1, tiled=True)
    grouped = received.reshape(-1, stn_count, tm_count, stations, 2 * spectra)
    real, imag = grams(grouped, 1.0 / (spectra * tm_count))
    return (real, imag)


def solution(mesh):
    return jax.shard_map(
        local,
        mesh=mesh,
        in_specs=(P(None, "stn", "tm"), P("stn"), P("stn"), P("stn"), P()),
        out_specs=(P(("stn", "tm"), None, None), P(("stn", "tm"), None, None)),
        check_vma=False,
    )
```
